768 devices in a mesh: row: 12 (over z_lo, x), col: 64 (over y, z_hi, core).
Axes of the slice: x: 4, y: 8, z: 12 (z_hi: 4, z_lo: 3; z = z_hi * 3 + z_lo), core: 2. Of those that a mesh axis runs over, the one named last changes fastest.
Arguments:
- grad_out: bfloat16 [98304, 128], P(('row', 'col')), may hold values from -6 to 6
- pre_act: bfloat16 [98304, 128], P(('row', 'col')), may hold values from -6 to 6
- features: bfloat16 [98304, 128], P(('row', 'col')), may hold values from -6 to 6
- weight: bfloat16 [128, 128], replicated, may hold values from -0.5 to 0.5
- blocks: bfloat16 [12, 64, 64, 2, 128, 128], P('row', 'col'), may hold values from -0.046875 to 0.046875
- block_cols: int32 [12, 64, 64, 2], P('row', 'col'), may hold values from 0 to 11
- block_counts: int32 [12, 64, 64], P('row', 'col'), may hold values from 0 to 2, as said below
- order: int32 [98304], P(('row', 'col')), may hold values from 0 to 127, as said below
Outputs:
- grad_feat: bfloat16 [98304, 128], P(('row', 'col'))
- weight_grad: float32 [128, 128], replicated
The draws below stay inside these ranges and needn't reach their ends.
Inputs may be any that keep to these rules, and one draw needn't show every extreme that they name: `block_counts`: every device's slice has at least one row block with 2 nonzero blocks. `order`: each slab of 128 entries is a permutation of 0 to 127.
All inputs are finite; a program needn't handle non-finite values.
Results may differ from the reference program's by a relative error of at most 0.019.
Values may be sent and summed in bfloat16 or wider, within the bound.
A program may use at most 64 MiB of HBM per device.

```python
import jax
import jax.numpy as jnp
from jax import lax

F = 128
B = 128
K = 2
BLK_DEV = 1
RB = 64
NCB = 12
NODES = 98304
N_ROW = 12
N_COL = 64


def draw_block_counts(key, part):
    key_level, key_trial, key_place = jax.random.split(jax.random.fold_in(key, 11), 3)
    level = jax.random.randint(key_level, (N_ROW, N_COL, 1, 1), 200, 1001)
    trials = jax.random.randint(key_trial, (N_ROW, N_COL, RB, K), 0, 1000)
    counts = jnp.sum((trials < level).astype(jnp.int32), axis=-1).astype(jnp.int32)
    place = jax.random.randint(key_place, (N_ROW, N_COL, 1), 0, RB)
    full_row = jnp.arange(RB, dtype=jnp.int32)[None, None, :] == place
    return jnp.where(full_row, K, counts).astype(jnp.int32)


def draw_order(key, part):
    slab_keys = jax.random.split(jax.random.fold_in(key, 23), N_ROW * N_COL)
    perms = jax.vmap(lambda single: jax.random.permutation(single, BLK_DEV * B))(slab_keys)
    return perms.reshape(-1).astype(jnp.int32)


def with_ends(result, own_key, least, high):
    longest = result.shape.index(max(result.shape))
    spots = []
    for shift in (0, 1):
        where = [jax.random.randint(jax.random.fold_in(own_key, axis), (), 0, length) for axis, length in enumerate(result.shape)]
        where[longest] = (where[longest] + shift) % result.shape[longest]
        spots.append(tuple(where))
    return result.at[spots[0]].set(least).at[spots[1]].set(high)


def shard_levels(key, shape, cuts, least, high):
    gain = 1.0
    for axis_at, blocks in cuts:
        steps = jax.random.uniform(jax.random.fold_in(jax.random.fold_in(key, 6), axis_at), (blocks,), jnp.float32, least / len(cuts), high / len(cuts))
        gain = gain * jnp.repeat(jnp.exp(steps), shape[axis_at] // blocks).reshape((-1,) + (1,) * (len(shape) - 1 - axis_at))
    return gain


def scatter_about(own_key, dims, width, reach, cuts=(), kind=jnp.bfloat16):
    drawn = jax.random.normal(own_key, dims, jnp.float32) * width
    if len(cuts) > 0:
        drawn = shard_levels(own_key, dims, cuts, -0.22, 0.18) * drawn
    return jnp.clip(drawn, min=-reach, max=reach).astype(kind)


def setup_inputs(seed: int = 0) -> dict:
    arg_keys = jax.random.split(jax.random.key(seed), 9)
    grad_out = scatter_about(arg_keys[0], (NODES, F), 1.0, 6.0, ((0, 768),))
    pre_act = scatter_about(arg_keys[1], (NODES, F), 1.0, 6.0, ((0, 768),))
    features = scatter_about(arg_keys[2], (NODES, F), 1.0, 6.0, ((0, 768),))
    weight = scatter_about(arg_keys[3], (F, F), F ** -0.5, 0.5)
    blocks = scatter_about(arg_keys[4], (N_ROW, N_COL, RB, K, B, B), (B * K * N_COL) ** -0.5, 0.046875, ((0, 12), (1, 64)))
    block_cols = with_ends(jax.random.randint(arg_keys[5], (N_ROW, N_COL, RB, K), 0, NCB), jax.random.fold_in(arg_keys[5], 1), 0, NCB - 1).astype(jnp.int32)
    block_counts = draw_block_counts(jax.random.fold_in(arg_keys[8], 71), 0)
    order = draw_order(jax.random.fold_in(arg_keys[8], 71), 0)
    return dict(grad_out=grad_out, pre_act=pre_act, features=features, weight=weight, blocks=blocks, block_cols=block_cols, block_counts=block_counts, order=order)


def reference(grad_out, pre_act, features, weight, blocks, block_cols, block_counts, order):
    slab_rows = BLK_DEV * B
    positions = ((jnp.arange(NODES, dtype=jnp.int32) // slab_rows) * slab_rows + order).astype(jnp.int32)
    masked = jnp.where(pre_act > 0, grad_out, jnp.zeros_like(grad_out))
    masked_block = masked[positions]
    feat_block = features[positions]
    panels = masked_block.reshape(N_ROW, RB, B, F)

    def device_term(carry, device):
        row_id = device // N_COL
        col_id = device % N_COL
        block_vals = blocks[row_id, col_id].astype(jnp.float32)
        panel_rows = panels[row_id].astype(jnp.float32)
        products = jnp.einsum("ikrc,irf->ikcf", block_vals, panel_rows, precision=lax.Precision.HIGHEST)
        filled = jnp.arange(K, dtype=jnp.int32)[None, :] < block_counts[row_id, col_id][:, None]
        hits = block_cols[row_id, col_id][:, :, None] == jnp.arange(NCB, dtype=jnp.int32)[None, None, :]
        selector = jnp.where(hits & filled[:, :, None], 1.0, 0.0).astype(jnp.float32)
        partial_value = jnp.einsum("ikj,ikcf->jcf", selector, products, precision=lax.Precision.HIGHEST)
        rounded = lax.optimization_barrier(partial_value.astype(jnp.bfloat16)).astype(jnp.float32)
        carry = carry.at[:, col_id].add(rounded.reshape(N_ROW, BLK_DEV, B, F))
        return carry, None

    zero_sum = jnp.zeros((N_ROW, N_COL, BLK_DEV, B, F), jnp.float32)
    summed, _ = lax.scan(device_term, zero_sum, jnp.arange(N_ROW * N_COL, dtype=jnp.int32))
    owned = summed.reshape(NODES, F).astype(jnp.bfloat16)
    grad_block = jnp.dot(owned, weight.T, preferred_element_type=jnp.float32).astype(jnp.bfloat16)
    grad_feat = jnp.zeros_like(features).at[positions].set(grad_block)
    weight_grad = jnp.dot(feat_block.T, owned, preferred_element_type=jnp.float32) * (NODES ** -0.5)
    return grad_feat, weight_grad
```

```python
import functools

import jax
import jax.numpy as jnp
from jax import lax
from jax.experimental import pallas as pl
from jax.experimental.pallas import tpu as pltpu
from jax.sharding import PartitionSpec as P

F = 128
B = 128
K = 2
NX = 4
NZL = 3
NY = 8
NZH = 4
NCORE = 2
ROWS = NZL * NX
COLS = NY * NZH * NCORE
MESH = pl.DeviceIdType.MESH


def col_of(y, zh, core):
    return (y * NZH + zh) * NCORE + core


def row_of(zl, x):
    return zl * NX + x


def place():
    row = lax.axis_index("row")
    col = lax.axis_index("col")
    zl = row // NX
    x = row % NX
    y = col // (NZH * NCORE)
    zh = (col // NCORE) % NZH
    core = col % NCORE
    return row, col, zl, x, y, zh, core


def remote(src, dst, ssem, rsem, row, col):
    return pltpu.make_async_remote_copy(
        src_ref=src,
        dst_ref=dst,
        send_sem=ssem,
        recv_sem=rsem,
        device_id=(row, col),
        device_id_type=MESH,
    )


def far(q):
    return q + q // 2 - 2 * (q // 3)


def one_hot(order_row):
    nodes = lax.broadcasted_iota(jnp.int32, (B, B), 0)
    return jnp.where(nodes == order_row, 1.0, 0.0).astype(jnp.bfloat16)


def gather_kernel(grad_ref, pre_ref, order_ref, reg, zs, zr, rs, rr, ls, lr, ps, pr):
    row, col, zl, x, y, zh, core = place()
    right = (y + 1) % NY
    left = (y + NY - 1) % NY
    partner = col_of(y, zh, 1 - core)

    barrier = pltpu.get_barrier_semaphore()
    peers = [col_of(right, zh, core), col_of(left, zh, core), partner]
    peers += [col_of(y, (zh + d) % NZH, core) for d in range(1, NZH)]
    for peer in peers:
        pl.semaphore_signal(barrier, inc=1, device_id=(row, peer), device_id_type=MESH)

    masked = jnp.where(pre_ref[...] > 0, grad_ref[...], jnp.zeros_like(grad_ref))
    own = lax.dot_general(
        masked,
        one_hot(order_ref[...]),
        (((0,), (0,)), ((), ())),
        preferred_element_type=jnp.float32,
    )
    reg[pl.ds(col, 1)] = own.astype(jnp.bfloat16)[None]
    pl.semaphore_wait(barrier, len(peers))

    def z_copy(d):
        return remote(
            reg.at[col], reg.at[col], zs.at[d - 1], zr.at[d - 1], row, col_of(y, (zh + d) % NZH, core)
        )

    for d in (1, 3, 2):
        z_copy(d).start()

    def slot(s, q):
        return col_of((y + NY + s) % NY, (zh + NZH - far(q)) % NZH, core)

    def view(index, s, forward):
        if s < NY // 2:
            return reg.at[index]
        return reg.at[index, pl.ds(0 if forward else B // 2, B // 2)]

    def r_copy(s, q):
        ref = view(slot(1 - s, q), s, True)
        return remote(ref, ref, rs.at[s - 1, q], rr.at[s - 1, q], row, col_of(right, zh, core))

    def l_copy(s, q):
        ref = view(slot(s - 1, q), s, False)
        return remote(ref, ref, ls.at[s - 1, q], lr.at[s - 1, q], row, col_of(left, zh, core))

    def got_r(s, q):
        ref = view(slot(-s, q), s, True)
        remote(ref, ref, rs.at[s - 1, q], rr.at[s - 1, q], row, col_of(right, zh, core)).wait_recv()

    def got_l(s, q):
        ref = view(slot(s, q), s, False)
        remote(ref, ref, ls.at[s - 1, q], lr.at[s - 1, q], row, col_of(left, zh, core)).wait_recv()

    def share(s, q):
        index = slot(s, q)
        remote(reg.at[index], reg.at[index], ps, pr, row, partner).start()

    for q in range(NZH):
        if q:
            d = (0, 1, 3, 2)[q]
            src = reg.at[slot(0, q)]
            remote(src, src, zs.at[d - 1], zr.at[d - 1], row, partner).wait_recv()
        r_copy(1, q).start()
        l_copy(1, q).start()
        share(0, q)

    half = NY // 2
    for s in range(1, half):

        def step(q, carry, s=s):
            got_r(s, q)
            r_copy(s + 1, q).start()
            share(-s, q)
            got_l(s, q)
            l_copy(s + 1, q).start()
            share(s, q)
            return carry

        lax.fori_loop(0, NZH, step, 0)

    def last(q, carry):
        got_r(half, q)
        got_l(half, q)
        share(half, q)
        return carry

    lax.fori_loop(0, NZH, last, 0)

    shared = reg.at[pl.ds(0, COLS // 2)]
    remote(shared, shared, ps, pr, row, partner).wait()
    for d in range(1, NZH):
        z_copy(d).wait_send()
    for s in range(1, half + 1):

        def sent(q, carry, s=s):
            r_copy(s, q).wait_send()
            l_copy(s, q).wait_send()
            return carry

        lax.fori_loop(0, NZH, sent, 0)


def gathered(grad_out, pre_act, order):
    return pl.pallas_call(
        gather_kernel,
        out_shape=jax.ShapeDtypeStruct((COLS, F, B), jnp.bfloat16),
        in_specs=[pl.BlockSpec(memory_space=pltpu.VMEM)] * 3,
        out_specs=pl.BlockSpec(memory_space=pltpu.VMEM),
        scratch_shapes=[
            pltpu.SemaphoreType.DMA((NZH - 1,)),
            pltpu.SemaphoreType.DMA((NZH - 1,)),
            pltpu.SemaphoreType.DMA((NY // 2, NZH)),
            pltpu.SemaphoreType.DMA((NY // 2, NZH)),
            pltpu.SemaphoreType.DMA((NY // 2, NZH)),
            pltpu.SemaphoreType.DMA((NY // 2, NZH)),
            pltpu.SemaphoreType.DMA,
            pltpu.SemaphoreType.DMA,
        ],
        compiler_params=pltpu.CompilerParams(collective_id=0, has_side_effects=True),
        name="gather",
    )(grad_out, pre_act, order)


TILE = 8


def product_kernel(target_ref, region_ref, blocks_ref, out_ref, acc, prod):
    step = pl.program_id(0)

    @pl.when(step == 0)
    def _():
        acc[...] = jnp.zeros_like(acc)

    for i in range(TILE):
        panel = region_ref[i]
        for k in range(K):
            prod[i * K + k] = jnp.dot(panel, blocks_ref[i, k], preferred_element_type=jnp.float32)
    for n in range(TILE * K):
        j = target_ref[step * (TILE * K) + n]
        acc[j] += prod[n]

    @pl.when(step == pl.num_programs(0) - 1)
    def _():
        out_ref[...] = acc[pl.ds(0, ROWS)].astype(jnp.bfloat16)


def partials(target, region, block_vals):
    count = block_vals.shape[0]
    return pl.pallas_call(
        product_kernel,
        out_shape=jax.ShapeDtypeStruct((ROWS, F, B), jnp.bfloat16),
        grid_spec=pltpu.PrefetchScalarGridSpec(
            num_scalar_prefetch=1,
            grid=(count // TILE,),
            in_specs=[
                pl.BlockSpec((TILE, F, B), lambda i, t: (i, 0, 0)),
                pl.BlockSpec((TILE, K, B, B), lambda i, t: (i, 0, 0, 0)),
            ],
            out_specs=pl.BlockSpec((ROWS, F, B), lambda i, t: (0, 0, 0)),
            scratch_shapes=[
                pltpu.VMEM((ROWS + 1, F, B), jnp.float32),
                pltpu.VMEM((TILE * K, F, B), jnp.float32),
            ],
        ),
        name="products",
    )(target, region, block_vals)


CHUNKS = NY * NCORE
CH = F // CHUNKS


def reduce_kernel(
    scale,
    part_ref,
    feat_ref,
    weight_ref,
    order_ref,
    grad_ref,
    wout_ref,
    rbuf,
    wsend,
    b1,
    b2,
    b3,
    b4,
    ssem,
    rsem,
):
    row, col, zl, x, y, zh, core = place()
    mine = y * NCORE + core
    z = zh * NZL + zl
    nz = NZL * NZH

    def row_peer(d):
        return (row + d) % ROWS, col

    def chunk_peer(d):
        q = (mine + d) % CHUNKS
        return row, col_of(q // NCORE, zh, q % NCORE)

    def z_peer(d):
        zz = (z + d) % nz
        return row_of(zz % NZL, x), col_of(y, zz // NZL, core)

    def x_peer(d):
        return row_of(zl, (x + d) % NX), col

    barrier = pltpu.get_barrier_semaphore()
    total = 0
    for peer, n in ((row_peer, ROWS), (chunk_peer, CHUNKS), (z_peer, nz), (x_peer, NX)):

        def greet(d, carry, peer=peer):
            pl.semaphore_signal(barrier, inc=1, device_id=peer(d), device_id_type=MESH)
            return carry

        lax.fori_loop(1, n, greet, 0)
        total += n - 1
    pl.semaphore_wait(barrier, total)

    def send_all(phase, n, src, dst, peer):
        def send(d, carry):
            r, c = peer(d)
            remote(src(d), dst(d), ssem.at[phase], rsem.at[phase], r, c).start()
            return carry

        lax.fori_loop(1, n, send, 0)

    def wait_all(phase, n, buf):
        ref = buf.at[pl.ds(0, n - 1)]
        remote(ref, ref, ssem.at[phase], rsem.at[phase], row, col).wait_recv()

    def wait_sent(phase, n, buf):
        ref = buf.at[pl.ds(0, n - 1)]
        remote(ref, ref, ssem.at[phase], rsem.at[phase], row, col).wait_send()

    send_all(0, ROWS, lambda d: part_ref.at[(row + d) % ROWS], lambda d: rbuf.at[d - 1], row_peer)
    total_sum = part_ref[row].astype(jnp.float32)
    wait_all(0, ROWS, rbuf)
    for d in range(ROWS - 1):
        total_sum += rbuf[d].astype(jnp.float32)
    owned_t = total_sum.astype(jnp.bfloat16)
    nodes = lax.dot_general(
        one_hot(order_ref[...]), owned_t, (((1,), (1,)), ((), ())), preferred_element_type=jnp.float32
    ).astype(jnp.bfloat16)
    partial_w = lax.dot_general(
        feat_ref[...], nodes, (((0,), (0,)), ((), ())), preferred_element_type=jnp.float32
    )
    wsend[...] = partial_w.reshape(CHUNKS, CH, F)

    def chunk_of(d):
        return (mine + d) % CHUNKS

    send_all(1, CHUNKS, lambda d: wsend.at[chunk_of(d)], lambda d: b1.at[d - 1], chunk_peer)
    grad_ref[...] = lax.dot_general(
        nodes, weight_ref[...], (((1,), (1,)), ((), ())), preferred_element_type=jnp.float32
    ).astype(jnp.bfloat16)
    wait_all(1, CHUNKS, b1)
    value = wsend[mine]
    for d in range(CHUNKS - 1):
        value += b1[d]
    b2[pl.ds(z, 1)] = value[None]
    send_all(2, nz, lambda d: b2.at[z], lambda d: b2.at[z], z_peer)
    wait_all(2, nz, b2)
    value = b2[0]
    for d in range(1, nz):
        value += b2[d]
    b3[pl.ds(x, 1)] = value[None]
    send_all(3, NX, lambda d: b3.at[x], lambda d: b3.at[x], x_peer)
    wait_all(3, NX, b3)
    value = b3[0]
    for d in range(1, NX):
        value += b3[d]
    b4[pl.ds(mine, 1)] = (value * scale)[None]
    send_all(4, CHUNKS, lambda d: b4.at[mine], lambda d: b4.at[mine], chunk_peer)
    wait_all(4, CHUNKS, b4)
    wout_ref[...] = b4[...].reshape(F, F)
    wait_sent(0, ROWS, rbuf)
    wait_sent(1, CHUNKS, b1)
    wait_sent(2, nz, b2)
    wait_sent(3, NX, b3)
    wait_sent(4, CHUNKS, b4)


def reduced(scale, part, features, weight, order):
    nz = NZL * NZH
    return pl.pallas_call(
        functools.partial(reduce_kernel, scale),
        out_shape=(
            jax.ShapeDtypeStruct((B, F), jnp.bfloat16),
            jax.ShapeDtypeStruct((F, F), jnp.float32),
        ),
        in_specs=[pl.BlockSpec(memory_space=pltpu.VMEM)] * 4,
        out_specs=(pl.BlockSpec(memory_space=pltpu.VMEM), pl.BlockSpec(memory_space=pltpu.VMEM)),
        scratch_shapes=[
            pltpu.VMEM((ROWS - 1, F, B), jnp.bfloat16),
            pltpu.VMEM((CHUNKS, CH, F), jnp.float32),
            pltpu.VMEM((CHUNKS - 1, CH, F), jnp.float32),
            pltpu.VMEM((nz, CH, F), jnp.float32),
            pltpu.VMEM((NX, CH, F), jnp.float32),
            pltpu.VMEM((CHUNKS, CH, F), jnp.float32),
            pltpu.SemaphoreType.DMA((5,)),
            pltpu.SemaphoreType.DMA((5,)),
        ],
        compiler_params=pltpu.CompilerParams(collective_id=1, has_side_effects=True),
        name="reduce",
    )(part, features, weight, order)


def shards(grad_out, pre_act, features, weight, blocks, block_cols, block_counts, order):
    order_row = order.reshape(1, B)
    region = gathered(grad_out, pre_act, order_row)
    filled = jnp.arange(K, dtype=jnp.int32)[None, :] < block_counts[0, 0][:, None]
    target = jnp.where(filled, block_cols[0, 0], ROWS).reshape(-1)
    part = partials(target, region, blocks[0, 0])
    scale = float(B * ROWS * COLS) ** -0.5
    return reduced(scale, part, features, weight, order_row)


def solution(mesh):
    placed = (
        P(("row", "col"), None),
        P(("row", "col"), None),
        P(("row", "col"), None),
        P(),
        P("row", "col", None, None, None, None),
        P("row", "col", None, None),
        P("row", "col", None),
        P(("row", "col")),
    )
    return jax.shard_map(
        shards,
        mesh=mesh,
        in_specs=placed,
        out_specs=(P(("row", "col"), None), P()),
        check_vma=False,
    )
```

```python
import functools

import jax
import jax.numpy as jnp
from jax import lax
from jax.experimental import pallas as pl
from jax.experimental.pallas import tpu as pltpu
from jax.sharding import PartitionSpec as P

F = 128
B = 128
K = 2
NX = 4
NZL = 3
NY = 8
NZH = 4
NCORE = 2
ROWS = NZL * NX
COLS = NY * NZH * NCORE
MESH = pl.DeviceIdType.MESH


def col_of(y, zh, core):
    return (y * NZH + zh) * NCORE + core


def row_of(zl, x):
    return zl * NX + x


def place():
    row = lax.axis_index("row")
    col = lax.axis_index("col")
    zl = row // NX
    x = row % NX
    y = col // (NZH * NCORE)
    zh = (col // NCORE) % NZH
    core = col % NCORE
    return row, col, zl, x, y, zh, core


def remote(src, dst, ssem, rsem, row, col):
    return pltpu.make_async_remote_copy(
        src_ref=src,
        dst_ref=dst,
        send_sem=ssem,
        recv_sem=rsem,
        device_id=(row, col),
        device_id_type=MESH,
    )


def far(q):
    return q + q // 2 - 2 * (q // 3)


def one_hot(order_row):
    nodes = lax.broadcasted_iota(jnp.int32, (B, B), 0)
    return jnp.where(nodes == order_row, 1.0, 0.0).astype(jnp.bfloat16)


CHUNKS = NY * NCORE
CH = F // CHUNKS
NZ = NZL * NZH
HALF = NY // 2
STAGES = tuple((t - o, q) for t in range(1, HALF + 3) for q, o in enumerate((0, 1, 1, 2)) if 1 <= t - o <= HALF)


def kernel(
    scale,
    cols_ref,
    counts_ref,
    grad_ref,
    pre_ref,
    order_ref,
    feat_ref,
    weight_ref,
    blocks_ref,
    gout_ref,
    wout_ref,
    reg,
    blk,
    run,
    prod,
    fbuf,
    part,
    rbuf,
    wsend,
    b1,
    b2,
    b3,
    b4,
    last,
    bsem,
    zs,
    zr,
    rs,
    rr,
    ls,
    lr,
    ps,
    pr,
    ssem,
    rsem,
):
    row, col, zl, x, y, zh, core = place()
    right = (y + 1) % NY
    left = (y + NY - 1) % NY
    partner = col_of(y, zh, 1 - core)
    mine = y * NCORE + core
    z = zh * NZL + zl

    def row_peer(d):
        return (row + d) % ROWS, col

    def chunk_peer(d):
        q = (mine + d) % CHUNKS
        return row, col_of(q // NCORE, zh, q % NCORE)

    def z_peer(d):
        zz = (z + d) % NZ
        return row_of(zz % NZL, x), col_of(y, zz // NZL, core)

    def x_peer(d):
        return row_of(zl, (x + d) % NX), col

    fetch = pltpu.make_async_copy(blocks_ref, blk, bsem)
    fetch.start()

    barrier = pltpu.get_barrier_semaphore()
    total = 0
    for peer, n in ((z_peer, NZ), (chunk_peer, CHUNKS), (row_peer, ROWS), (x_peer, NX)):

        def greet(d, carry, peer=peer):
            pl.semaphore_signal(barrier, inc=1, device_id=peer(d), device_id_type=MESH)
            return carry

        lax.fori_loop(1, n, greet, 0)
        total += n - 1

    masked = jnp.where(pre_ref[...] > 0, grad_ref[...], jnp.zeros_like(grad_ref))
    hot = one_hot(order_ref[...])
    own = lax.dot_general(masked, hot, (((0,), (0,)), ((), ())), preferred_element_type=jnp.float32)
    reg[pl.ds(col, 1)] = own.astype(jnp.bfloat16)[None]
    feat = lax.dot_general(hot, feat_ref[...], (((0,), (0,)), ((), ())), preferred_element_type=jnp.float32)
    fbuf[pl.ds(row, 1)] = feat.astype(jnp.bfloat16)[None]
    run[COLS * K] = jnp.zeros((F, B), jnp.float32)
    for j in range(ROWS):
        last[j] = COLS * K
    pl.semaphore_wait(barrier, total)

    def send_all(phase, n, src, dst, peer):
        def send(d, carry):
            r, c = peer(d)
            remote(src(d), dst(d), ssem.at[phase], rsem.at[phase], r, c).start()
            return carry

        lax.fori_loop(1, n, send, 0)

    def wait_all(phase, n, buf):
        ref = buf.at[pl.ds(0, n - 1)]
        remote(ref, ref, ssem.at[phase], rsem.at[phase], row, partner).wait_recv()

    def wait_sent(phase, n, buf):
        ref = buf.at[pl.ds(0, n - 1)]
        remote(ref, ref, ssem.at[phase], rsem.at[phase], row, partner).wait_send()

    def z_copy(d):
        return remote(
            reg.at[col], reg.at[col], zs.at[d - 1], zr.at[d - 1], row, col_of(y, (zh + d) % NZH, core)
        )

    def slot(s, q, c=None):
        return col_of((y + NY + s) % NY, (zh + NZH - far(q)) % NZH, core if c is None else c)

    def view(index, s, forward):
        if s < HALF:
            return reg.at[index]
        return reg.at[index, pl.ds(0 if forward else F // 2, F // 2)]

    def r_copy(s, q):
        ref = view(slot(1 - s, q), s, True)
        return remote(ref, ref, rs.at[s - 1, q], rr.at[s - 1, q], row, col_of(right, zh, core))

    def l_copy(s, q):
        ref = view(slot(s - 1, q), s, False)
        return remote(ref, ref, ls.at[s - 1, q], lr.at[s - 1, q], row, col_of(left, zh, core))

    def got_r(s, q):
        ref = view(slot(-s, q), s, True)
        remote(ref, ref, rs.at[s - 1, q], rr.at[s - 1, q], row, col_of(right, zh, core)).wait_recv()

    def got_l(s, q):
        ref = view(slot(s, q), s, False)
        remote(ref, ref, ls.at[s - 1, q], lr.at[s - 1, q], row, col_of(left, zh, core)).wait_recv()

    def share(s, q):
        ref = reg.at[slot(s, q)]
        return remote(ref, ref, ps.at[s + HALF - 1, q], pr.at[s + HALF - 1, q], row, partner)

    def got_share(s, q):
        ref = reg.at[slot(s, q, 1 - core)]
        remote(ref, ref, ps.at[s + HALF - 1, q], pr.at[s + HALF - 1, q], row, partner).wait_recv()

    def process(indices):
        for n, i in enumerate(indices):
            panel = reg[i]
            for k in range(K):
                prod[n * K + k] = jnp.dot(panel, blk[i, k], preferred_element_type=jnp.float32)
        for n, i in enumerate(indices):
            for k in range(K):
                j = jnp.where(k < counts_ref[0, i], cols_ref[k, i], ROWS)
                before = [last[t] for t in range(ROWS)]
                prev = jnp.int32(COLS * K)
                for t in range(ROWS):
                    prev = jnp.where(j == t, before[t], prev)
                at = i * K + k
                run[at] = prod[n * K + k] + run[prev]
                for t in range(ROWS):
                    last[t] = jnp.where(j == t, at, before[t])

    def offsets(s):
        return (s,) if s in (0, HALF) else (-s, s)

    def start(q):
        if q:
            d = (0, 1, 3, 2)[q]
            ref = reg.at[slot(0, q)]
            remote(ref, ref, zs.at[d - 1], zr.at[d - 1], row, partner).wait_recv()
        r_copy(1, q).start()
        l_copy(1, q).start()
        share(0, q).start()

    done = []

    def drain(s, q):
        indices = [slot(o, q) for o in offsets(s)]
        if done:
            ps_, pq_ = done[-1]
            for o in offsets(ps_):
                got_share(o, pq_)
                indices.append(slot(o, pq_, 1 - core))
        done.append((s, q))
        process(indices)

    for d in (1, 3, 2):
        z_copy(d).start()
    start(0)
    fetch.wait()
    drain(0, 0)
    for s, q in STAGES:
        got_r(s, q)
        if s < HALF:
            r_copy(s + 1, q).start()
        if s < HALF:
            share(-s, q).start()
        got_l(s, q)
        if s < HALF:
            l_copy(s + 1, q).start()
        share(s, q).start()
        if (s, q) == (1, 0):
            start(1)
            start(2)
            send_all(5, ROWS, lambda d: fbuf.at[row], lambda d: fbuf.at[row], row_peer)
            drain(s, q)
            drain(0, 1)
            drain(0, 2)
        elif (s, q) == (1, 2):
            start(3)
            drain(s, q)
            drain(0, 3)
        else:
            drain(s, q)
    s, q = done[-1]
    rest = []
    for o in offsets(s):
        got_share(o, q)
        rest.append(slot(o, q, 1 - core))
    process(rest)

    for j in range(ROWS):
        part[j] = run[last[j]].astype(jnp.bfloat16)
    send_all(0, ROWS, lambda d: part.at[(row + d) % ROWS], lambda d: rbuf.at[d - 1], row_peer)
    wait_all(5, ROWS, fbuf)
    weight_sum = jnp.zeros((F, F), jnp.float32)
    for j in range(ROWS):
        weight_sum += jnp.dot(part[j], fbuf[j], preferred_element_type=jnp.float32)
    wsend[...] = weight_sum.reshape(CHUNKS, CH, F)
    send_all(1, CHUNKS, lambda d: wsend.at[(mine + d) % CHUNKS], lambda d: b1.at[d - 1], chunk_peer)

    wait_all(1, CHUNKS, b1)
    value = wsend[mine]
    for d in range(CHUNKS - 1):
        value += b1[d]
    b2[pl.ds(z, 1)] = value[None]
    send_all(2, NZ, lambda d: b2.at[z], lambda d: b2.at[z], z_peer)

    wait_all(0, ROWS, rbuf)
    owned = part[row].astype(jnp.float32)
    for d in range(ROWS - 1):
        owned += rbuf[d].astype(jnp.float32)
    nodes = lax.dot_general(
        one_hot(order_ref[...]),
        owned.astype(jnp.bfloat16),
        (((1,), (1,)), ((), ())),
        preferred_element_type=jnp.float32,
    ).astype(jnp.bfloat16)
    gout_ref[...] = lax.dot_general(
        nodes, weight_ref[...], (((1,), (1,)), ((), ())), preferred_element_type=jnp.float32
    ).astype(jnp.bfloat16)

    wait_all(2, NZ, b2)
    value = b2[0]
    for d in range(1, NZ):
        value += b2[d]
    b3[pl.ds(x, 1)] = value[None]
    send_all(3, NX, lambda d: b3.at[x], lambda d: b3.at[x], x_peer)

    for d in range(1, NZH):
        z_copy(d).wait_send()
    for s in range(1, HALF + 1):

        def sent(q, carry, s=s):
            r_copy(s, q).wait_send()
            l_copy(s, q).wait_send()
            return carry

        lax.fori_loop(0, NZH, sent, 0)
    for s in range(1 - HALF, HALF + 1):

        def given(q, carry, s=s):
            share(s, q).wait_send()
            return carry

        lax.fori_loop(0, NZH, given, 0)
    wait_sent(5, ROWS, fbuf)
    wait_sent(0, ROWS, rbuf)
    wait_sent(1, CHUNKS, b1)
    wait_sent(2, NZ, b2)

    wait_all(3, NX, b3)
    value = b3[0]
    for d in range(1, NX):
        value += b3[d]
    b4[pl.ds(mine, 1)] = (value * scale)[None]
    send_all(4, CHUNKS, lambda d: b4.at[mine], lambda d: b4.at[mine], chunk_peer)
    wait_all(4, CHUNKS, b4)
    wout_ref[...] = b4[...].reshape(F, F)
    wait_sent(3, NX, b3)
    wait_sent(4, CHUNKS, b4)


def whole(scale, cols, counts, grad_out, pre_act, order, features, weight, block_vals):
    vmem = pl.BlockSpec(memory_space=pltpu.VMEM)
    smem = pl.BlockSpec(memory_space=pltpu.SMEM)
    dma = pltpu.SemaphoreType.DMA
    return pl.pallas_call(
        functools.partial(kernel, scale),
        out_shape=(
            jax.ShapeDtypeStruct((B, F), jnp.bfloat16),
            jax.ShapeDtypeStruct((F, F), jnp.float32),
        ),
        in_specs=[smem, smem, vmem, vmem, vmem, vmem, vmem, pl.BlockSpec(memory_space=pl.ANY)],
        out_specs=(vmem, vmem),
        scratch_shapes=[
            pltpu.VMEM((COLS, F, B), jnp.bfloat16),
            pltpu.VMEM((COLS, K, B, B), jnp.bfloat16),
            pltpu.VMEM((COLS * K + 1, F, B), jnp.float32),
            pltpu.VMEM((4 * K, F, B), jnp.float32),
            pltpu.VMEM((ROWS, B, F), jnp.bfloat16),
            pltpu.VMEM((ROWS, F, B), jnp.bfloat16),
            pltpu.VMEM((ROWS - 1, F, B), jnp.bfloat16),
            pltpu.VMEM((CHUNKS, CH, F), jnp.float32),
            pltpu.VMEM((CHUNKS - 1, CH, F), jnp.float32),
            pltpu.VMEM((NZ, CH, F), jnp.float32),
            pltpu.VMEM((NX, CH, F), jnp.float32),
            pltpu.VMEM((CHUNKS, CH, F), jnp.float32),
            pltpu.SMEM((ROWS,), jnp.int32),
            dma,
            dma((NZH - 1,)),
            dma((NZH - 1,)),
            dma((HALF, NZH)),
            dma((HALF, NZH)),
            dma((HALF, NZH)),
            dma((HALF, NZH)),
            dma((NY, NZH)),
            dma((NY, NZH)),
            dma((6,)),
            dma((6,)),
        ],
        compiler_params=pltpu.CompilerParams(
            collective_id=0, has_side_effects=True, vmem_limit_bytes=40 * 1024 * 1024
        ),
        name="whole",
    )(cols, counts, grad_out, pre_act, order, features, weight, block_vals)


def shards(grad_out, pre_act, features, weight, blocks, block_cols, block_counts, order):
    scale = float(B * ROWS * COLS) ** -0.5
    grad_feat, weight_t = whole(
        scale,
        block_cols[0, 0].T,
        block_counts[0],
        grad_out,
        pre_act,
        order.reshape(1, B),
        features,
        weight,
        blocks[0, 0],
    )
    return grad_feat, weight_t.T


def solution(mesh):
    placed = (
        P(("row", "col"), None),
        P(("row", "col"), None),
        P(("row", "col"), None),
        P(),
        P("row", "col", None, None, None, None),
        P("row", "col", None, None),
        P("row", "col", None),
        P(("row", "col")),
    )
    return jax.shard_map(
        shards,
        mesh=mesh,
        in_specs=placed,
        out_specs=(P(("row", "col"), None), P()),
        check_vma=False,
    )
```
